512 devices in a mesh: guide: 2 (over core), patch: 256 (over x, y, z).
Axes of the slice: x: 4, y: 4, z: 16, core: 2. Of those that a mesh axis runs over, the one named last changes fastest.
Arguments:
- queries: bfloat16 [2, 28672, 128], P('guide', 'patch'), may hold values from -40 to 40
- fresh_keys: bfloat16 [2, 28672, 128], P('guide', 'patch'), may hold values from -9.5625 to 9.5625
- fresh_values: bfloat16 [2, 28672, 128], P('guide', 'patch'), may hold values from -6 to 6
- stale_keys: bfloat16 [2, 28672, 128], P('guide', 'patch'), may hold values from -10 to 10
- stale_values: bfloat16 [2, 28672, 128], P('guide', 'patch'), may hold values from -6 to 6
- hidden: bfloat16 [2, 28672, 5120], P('guide', 'patch'), may hold values from -6 to 6
- out_weight: bfloat16 [128, 5120], replicated, may hold values from -0.5 to 0.5
- modulation: float32 [5120], replicated, may hold values from 1 to 4
Outputs:
- guided: bfloat16 [28672, 5120], P('patch', 'guide')
The draws below stay inside these ranges and needn't reach their ends.
All inputs are finite; a program needn't handle non-finite values.
Results may differ from the reference program's by a relative error of at most 0.0051.
Values may be sent and summed in bfloat16 or wider, within the bound.
No kernel may reach another device: no remote copies, remote signals or barrier semaphores. Data moves between devices by JAX's collectives and lax.ppermute only.
A program may use at most 64 MiB of HBM per device.

```python
import math
import jax
import jax.numpy as jnp
from jax import lax

D = 5120
HD = 128
TOK_DEV = 112
TOKENS = 28672
N_PATCH = 256


SPREAD = 1.6


def joint_draw(key):
    base = jax.random.fold_in(key, 11)
    key_first, key_second = jax.random.split(base)
    shape = (2, TOKENS, HD)
    old_keys = jnp.clip(jax.random.normal(key_first, shape, jnp.float32) * SPREAD, -9.6, 9.6)
    query_rows = jnp.clip(jax.random.normal(key_second, shape, jnp.float32) * SPREAD, -9.6, 9.6)
    return (query_rows, old_keys)


def draw_queries(key, part):
    return joint_draw(key)[0].astype(jnp.bfloat16)


def draw_stale_keys(key, part):
    return joint_draw(key)[1].astype(jnp.bfloat16)


def block_scale(key, shape, shards, least, largest):
    factor_of, own = 1.0, jax.random.fold_in(key, 6)
    for position, shards_of in shards:
        heights = jnp.exp(jax.random.uniform(jax.random.fold_in(own, position), (shards_of,), jnp.float32, least / len(shards), largest / len(shards)))
        factor_of = factor_of * jnp.repeat(heights, shape[position] // shards_of).reshape([-1 if axis == position else 1 for axis in range(len(shape))])
    return factor_of


def scatter_about(own_key, dims, deviation, bound, cuts=(), held_as=jnp.bfloat16):
    level = block_scale(own_key, dims, cuts, -0.22, 0.18) if cuts else 1.0
    entries = jax.random.normal(own_key, dims, jnp.float32) * deviation * level
    return jnp.minimum(jnp.maximum(entries, -bound), bound).astype(held_as)


def setup_inputs(seed: int = 0) -> dict:
    arg_keys = jax.random.split(jax.random.key(seed), 9)
    queries = draw_queries(jax.random.fold_in(arg_keys[8], 71), 0)
    fresh_keys = scatter_about(arg_keys[1], (2, TOKENS, HD), 1.6, 9.5625, ((0, 2), (1, 256)))
    fresh_values = scatter_about(arg_keys[2], (2, TOKENS, HD), 1.0, 6.0, ((0, 2), (1, 256)))
    stale_keys = draw_stale_keys(jax.random.fold_in(arg_keys[8], 71), 0)
    stale_values = scatter_about(arg_keys[4], (2, TOKENS, HD), 1.0, 6.0, ((0, 2), (1, 256)))
    hidden = scatter_about(arg_keys[5], (2, TOKENS, D), 1.0, 6.0, ((0, 2), (1, 256)))
    out_weight = scatter_about(arg_keys[6], (HD, D), HD ** -0.5, 0.5)
    modulation = jnp.clip(jnp.exp(jax.random.uniform(arg_keys[7], (D,), jnp.float32, math.log(1.0), math.log(4.0))), 1.0, 4.0)
    return {"queries": queries, "fresh_keys": fresh_keys, "fresh_values": fresh_values, "stale_keys": stale_keys, "stale_values": stale_values, "hidden": hidden, "out_weight": out_weight, "modulation": modulation}


def reference(queries, fresh_keys, fresh_values, stale_keys, stale_values, hidden, out_weight, modulation):
    score_scale = 1.0 / math.sqrt(HD)
    outputs = []
    for branch in range(2):

        def one_patch(patch_index):
            first_row = (patch_index * TOK_DEV).astype(jnp.int32)
            new_keys = lax.dynamic_slice_in_dim(fresh_keys[branch], first_row, TOK_DEV, 0)
            new_values = lax.dynamic_slice_in_dim(fresh_values[branch], first_row, TOK_DEV, 0)
            key_rows = lax.dynamic_update_slice_in_dim(stale_keys[branch], new_keys, first_row, 0)
            value_rows = lax.dynamic_update_slice_in_dim(stale_values[branch], new_values, first_row, 0)
            query_rows = lax.dynamic_slice_in_dim(queries[branch], first_row, TOK_DEV, 0)
            scores = jnp.dot(query_rows, key_rows.T, preferred_element_type=jnp.float32) * score_scale
            peak = lax.optimization_barrier(jnp.max(scores, axis=1, keepdims=True))
            weights = jnp.exp(scores - peak).astype(jnp.bfloat16)
            total = lax.optimization_barrier(jnp.sum(weights.astype(jnp.float32), axis=1))
            summed = jnp.dot(weights, value_rows, preferred_element_type=jnp.float32)
            attention = (summed / total[:, None]).astype(jnp.bfloat16)
            projected = jnp.dot(attention, out_weight, preferred_element_type=jnp.float32)
            residual = lax.dynamic_slice_in_dim(hidden[branch], first_row, TOK_DEV, 0)
            return (residual.astype(jnp.float32) + modulation[None, :] * projected).astype(jnp.bfloat16)
        mapped = lax.map(one_patch, jnp.arange(N_PATCH, dtype=jnp.int32))
        outputs.append(mapped.reshape(TOKENS, D))
    conditional = outputs[0].astype(jnp.float32)
    unconditional = outputs[1].astype(jnp.float32)
    return (unconditional + 5.0 * (conditional - unconditional)).astype(jnp.bfloat16)
```

```python
import functools
import math

import jax
import jax.numpy as jnp
from jax import lax
from jax.experimental import pallas as pl
from jax.experimental.pallas import tpu as pltpu
from jax.sharding import Mesh
from jax.sharding import PartitionSpec as P

GUIDANCE = 5.0
AXES = ("x", "y", "z")
SIZES = (4, 4, 16)
QUERY_AXES = ("x", "y")
KEY_AXES = ("z",)
STATS = 16


def attend_kernel(place, query, cached, fresh, out, keys, values):
    step = pl.program_id(0)
    steps = pl.num_programs(0)
    rows = query.shape[1]
    head = query.shape[2]
    scale = 1.0 / math.sqrt(head)

    @pl.when(step == 0)
    def _():
        keys[...] = cached[:, :head]
        values[:, :head] = cached[:, head:]
        values[:, head:] = jnp.ones((values.shape[0], head), values.dtype)

    @pl.when(step == steps - 1)
    def _():
        own = pl.ds(pl.multiple_of(place[1] * rows, rows), rows)
        keys[own, :] = fresh[:, :head]
        values[own, :head] = fresh[:, head:]

    scores = lax.dot_general(
        query[0], keys[...], (((1,), (1,)), ((), ())), preferred_element_type=jnp.float32
    )
    peak = jnp.max(scores, axis=1, keepdims=True)
    weights = jnp.exp2((scores - peak) * (scale * math.log2(math.e))).astype(jnp.bfloat16)
    summed = jnp.dot(weights, values[...], preferred_element_type=jnp.float32)
    total = summed[:, head:]
    out[0, :rows, :] = (summed[:, :head] / total).astype(out.dtype)
    level = peak * scale + jnp.log(total)
    level = jnp.concatenate([level, jnp.zeros((head - rows, head), jnp.float32)], axis=0)
    level = level.T[:STATS]
    high = level.astype(jnp.bfloat16).astype(jnp.float32)
    middle = (level - high).astype(jnp.bfloat16).astype(jnp.float32)
    low = level - high - middle
    row = lax.broadcasted_iota(jnp.int32, level.shape, 0)
    stats = jnp.where(row == 0, high, jnp.where(row == 1, middle, low))
    out[0, rows:, :] = stats.astype(out.dtype)


def attend(place, queries, cached, fresh):
    steps, rows, head = queries.shape
    key_rows = cached.shape[0]

    def turn(step, place):
        return (lax.rem(place[0] + 1 + step, steps), 0, 0)

    return pl.pallas_call(
        attend_kernel,
        out_shape=jax.ShapeDtypeStruct((steps, rows + STATS, head), jnp.bfloat16),
        grid_spec=pltpu.PrefetchScalarGridSpec(
            num_scalar_prefetch=1,
            grid=(steps,),
            in_specs=[
                pl.BlockSpec((1, rows, head), turn),
                pl.BlockSpec((key_rows, 2 * head), lambda step, place: (0, 0)),
                pl.BlockSpec((rows, 2 * head), lambda step, place: (0, 0)),
            ],
            out_specs=pl.BlockSpec((1, rows + STATS, head), turn),
            scratch_shapes=[
                pltpu.VMEM((key_rows, head), jnp.bfloat16),
                pltpu.VMEM((key_rows, 2 * head), jnp.bfloat16),
            ],
        ),
        compiler_params=pltpu.CompilerParams(dimension_semantics=("arbitrary",)),
        name="attend",
    )(place, queries, cached, fresh)


def project(attention, hidden, weight, gain):
    projected = jnp.dot(attention, weight, preferred_element_type=jnp.float32)
    return (hidden.astype(jnp.float32) + gain * projected).astype(jnp.bfloat16)


def merge_kernel(place, parts, hidden, weight, gain, attention, out):
    count = parts.shape[0]
    rows = hidden.shape[0]
    head = parts.shape[2]
    levels = []
    for part in range(count):
        pieces = parts[part, rows:, :].astype(jnp.float32)
        levels.append(pieces[0:1] + pieces[1:2] + pieces[2:3])
    level = jnp.concatenate(levels, axis=0)
    share = jnp.exp(level - jnp.max(level, axis=0, keepdims=True))
    share = share / jnp.sum(share, axis=0, keepdims=True)
    share = jnp.concatenate([share, jnp.zeros((head - count, head), jnp.float32)], axis=0).T
    merged = jnp.zeros((rows, head), jnp.float32)
    for part in range(count):
        merged += parts[part, :rows, :].astype(jnp.float32) * share[:rows, part : part + 1]
    merged = merged.astype(jnp.bfloat16)
    attention[...] = merged
    out[...] = project(merged, hidden[...], weight[...], gain[...])


def merge(place, parts, hidden, weight, gain):
    count, padded, head = parts.shape
    rows, width = hidden.shape
    half = width // 2

    def other(step, place):
        return (0, 1 - place[2])

    return pl.pallas_call(
        merge_kernel,
        out_shape=[
            jax.ShapeDtypeStruct((rows, head), jnp.bfloat16),
            jax.ShapeDtypeStruct((rows, half), jnp.bfloat16),
        ],
        grid_spec=pltpu.PrefetchScalarGridSpec(
            num_scalar_prefetch=1,
            grid=(1,),
            in_specs=[
                pl.BlockSpec((count, padded, head), lambda step, place: (0, 0, 0)),
                pl.BlockSpec((rows, half), other),
                pl.BlockSpec((head, half), other),
                pl.BlockSpec((1, half), other),
            ],
            out_specs=[
                pl.BlockSpec((rows, head), lambda step, place: (0, 0)),
                pl.BlockSpec((rows, half), lambda step, place: (0, 0)),
            ],
        ),
        name="merge",
    )(place, parts, hidden, weight, gain)


def own_kernel(place, attention, hidden, weight, gain, out):
    out[...] = project(attention[...], hidden[...], weight[...], gain[...])


def own_half(place, attention, hidden, weight, gain):
    rows, width = hidden.shape
    head = attention.shape[1]
    half = width // 2

    def mine(step, place):
        return (0, place[2])

    return pl.pallas_call(
        own_kernel,
        out_shape=jax.ShapeDtypeStruct((rows, half), jnp.bfloat16),
        grid_spec=pltpu.PrefetchScalarGridSpec(
            num_scalar_prefetch=1,
            grid=(1,),
            in_specs=[
                pl.BlockSpec((rows, head), lambda step, place: (0, 0)),
                pl.BlockSpec((rows, half), mine),
                pl.BlockSpec((head, half), mine),
                pl.BlockSpec((1, half), mine),
            ],
            out_specs=pl.BlockSpec((rows, half), lambda step, place: (0, 0)),
        ),
        cost_estimate=pl.CostEstimate(
            flops=2 * rows * head * half, bytes_accessed=4 * rows * half, transcendentals=0
        ),
        name="own_half",
    )(place, attention, hidden, weight, gain)


def on_device(
    queries, fresh_keys, fresh_values, stale_keys, stale_values, hidden, out_weight, modulation
):
    side = lax.axis_index("guide")
    place = jnp.stack(
        [lax.axis_index(QUERY_AXES), lax.axis_index(KEY_AXES), side]
    ).astype(jnp.int32)
    query_group = lax.axis_size(QUERY_AXES)
    cached = jnp.concatenate([stale_keys[0], stale_values[0]], axis=1)
    fresh = jnp.concatenate([fresh_keys[0], fresh_values[0]], axis=1)
    spread = jnp.broadcast_to(queries, (query_group,) + queries.shape[1:])
    group_queries = lax.all_to_all(spread, QUERY_AXES, 0, 0)
    group_cached = lax.all_gather(cached, KEY_AXES, axis=0, tiled=True)
    partials = attend(place, group_queries, group_cached, fresh)
    parts = lax.all_to_all(partials, QUERY_AXES, 0, 0)
    gain = modulation[None, :]
    attention, sent = merge(place, parts, hidden[0], out_weight, gain)
    partner = lax.ppermute(sent, "guide", [(0, 1), (1, 0)])
    own = own_half(place, attention, hidden[0], out_weight, gain)
    own_value = own.astype(jnp.float32)
    partner_value = partner.astype(jnp.float32)
    conditional = jnp.where(side == 0, own_value, partner_value)
    unconditional = jnp.where(side == 0, partner_value, own_value)
    return (unconditional + GUIDANCE * (conditional - unconditional)).astype(jnp.bfloat16)


def solution(mesh):
    split = Mesh(mesh.devices.reshape((mesh.shape["guide"],) + SIZES), ("guide",) + AXES)
    rows = P("guide", AXES, None)
    return jax.shard_map(
        on_device,
        mesh=split,
        in_specs=(rows,) * 6 + (P(), P()),
        out_specs=P(AXES, "guide"),
        check_vma=False,
    )
```

```python
import math

import jax
import jax.numpy as jnp
from jax import lax
from jax.experimental import pallas as pl
from jax.experimental.pallas import tpu as pltpu
from jax.sharding import Mesh
from jax.sharding import PartitionSpec as P

GUIDANCE = 5.0
AXES = ("x", "y", "z")
SIZES = (4, 4, 16)
QUERY_AXES = ("x", "y")
KEY_AXES = ("z",)
STATS = 16
TOGETHER = 2
VMEM = pl.BlockSpec(memory_space=pltpu.VMEM)
SMEM = pl.BlockSpec(memory_space=pltpu.SMEM)


def write_part(out, index, summed, total, peak, scale):
    rows, head = summed.shape
    out[index, :rows, :] = (summed / total).astype(out.dtype)
    level = peak * scale + jnp.log(total)
    level = jnp.concatenate([level, jnp.zeros((head - rows, head), jnp.float32)], axis=0)
    level = level.T[:STATS]
    high = level.astype(jnp.bfloat16).astype(jnp.float32)
    middle = (level - high).astype(jnp.bfloat16).astype(jnp.float32)
    low = level - high - middle
    row = lax.broadcasted_iota(jnp.int32, level.shape, 0)
    stats = jnp.where(row == 0, high, jnp.where(row == 1, middle, low))
    out[index, rows:, :] = stats.astype(out.dtype)


def prepare_kernel(cached, keys, values):
    head = keys.shape[0]
    keys[...] = cached[:, :head].T
    values[:, :head] = cached[:, head:]
    values[:, head:] = jnp.ones((values.shape[0], head), values.dtype)


def prepare(cached):
    rows, width = cached.shape
    return pl.pallas_call(
        prepare_kernel,
        out_shape=[
            jax.ShapeDtypeStruct((width // 2, rows), cached.dtype),
            jax.ShapeDtypeStruct((rows, width), cached.dtype),
        ],
        in_specs=[VMEM],
        out_specs=[VMEM] * 2,
        compiler_params=pltpu.CompilerParams(vmem_limit_bytes=12 << 20),
        name="prepare",
    )(cached)


def attend_kernel(query, keys, values, out):
    count, rows, head = query.shape
    scale = 1.0 / math.sqrt(head)
    for first in range(0, count, TOGETHER):
        block = query[first : first + TOGETHER].reshape(TOGETHER * rows, head)
        scores = jnp.dot(block, keys[...], preferred_element_type=jnp.float32)
        peak = jnp.max(scores, axis=1, keepdims=True)
        weights = jnp.exp2((scores - peak) * (scale * math.log2(math.e))).astype(jnp.bfloat16)
        summed = jnp.dot(weights, values[...], preferred_element_type=jnp.float32)
        for k in range(TOGETHER):
            part = slice(k * rows, (k + 1) * rows)
            write_part(out, first + k, summed[part, :head], summed[part, head:], peak[part], scale)


def attend(queries, keys, values):
    count, rows, head = queries.shape
    size = count * rows * keys.shape[1]
    return pl.pallas_call(
        attend_kernel,
        out_shape=jax.ShapeDtypeStruct((count, rows + STATS, head), jnp.bfloat16),
        in_specs=[VMEM] * 3,
        out_specs=VMEM,
        cost_estimate=pl.CostEstimate(
            flops=6 * size * head, bytes_accessed=8 * keys.size, transcendentals=size
        ),
        compiler_params=pltpu.CompilerParams(vmem_limit_bytes=24 << 20),
        name="attend",
    )(queries, keys, values)


def attend_own_kernel(place, query, keys, values, fresh, out):
    rows, head = query.shape
    scale = 1.0 / math.sqrt(head)
    contract = (((1,), (1,)), ((), ()))
    stale = jnp.dot(query[...], keys[...], preferred_element_type=jnp.float32)
    column = lax.broadcasted_iota(jnp.int32, stale.shape, 1) - place[1] * rows
    stale = jnp.where((column >= 0) & (column < rows), -jnp.inf, stale)
    new = lax.dot_general(
        query[...], fresh[:, :head], contract, preferred_element_type=jnp.float32
    )
    peak = jnp.maximum(
        jnp.max(stale, axis=1, keepdims=True), jnp.max(new, axis=1, keepdims=True)
    )
    factor = scale * math.log2(math.e)
    stale = jnp.exp2((stale - peak) * factor).astype(jnp.bfloat16)
    new = jnp.exp2((new - peak) * factor).astype(jnp.bfloat16)
    both = jnp.dot(stale, values[...], preferred_element_type=jnp.float32)
    total = both[:, head:] + jnp.sum(new.astype(jnp.float32), axis=1, keepdims=True)
    summed = both[:, :head] + jnp.dot(
        new, fresh[:, head:], preferred_element_type=jnp.float32
    )
    write_part(out, 0, summed, total, peak, scale)


def attend_own(place, query, keys, values, fresh):
    rows, head = query.shape
    size = rows * keys.shape[1]
    return pl.pallas_call(
        attend_own_kernel,
        out_shape=jax.ShapeDtypeStruct((1, rows + STATS, head), jnp.bfloat16),
        in_specs=[SMEM] + [VMEM] * 4,
        out_specs=VMEM,
        cost_estimate=pl.CostEstimate(
            flops=6 * size * head, bytes_accessed=8 * keys.size, transcendentals=size
        ),
        compiler_params=pltpu.CompilerParams(vmem_limit_bytes=12 << 20),
        name="attend_own",
    )(place, query, keys, values, fresh)


def project(attention, hidden, weight, gain):
    projected = jnp.dot(attention, weight, preferred_element_type=jnp.float32)
    return (hidden.astype(jnp.float32) + gain * projected).astype(jnp.bfloat16)


def level_of(part, rows):
    pieces = part[rows:, :].astype(jnp.float32)
    return pieces[0:1] + pieces[1:2] + pieces[2:3]


def merge_kernel(place, parts, own, hidden, weight, gain, attention, out):
    count = parts.shape[0]
    rows = hidden.shape[0]
    head = parts.shape[2]
    levels = []
    for part in range(count):
        level = level_of(parts[part], rows)
        levels.append(jnp.where(place[0] == part, -jnp.inf, level))
    levels.append(level_of(own[0], rows))
    level = jnp.concatenate(levels, axis=0)
    share = jnp.exp(level - jnp.max(level, axis=0, keepdims=True))
    share = share / jnp.sum(share, axis=0, keepdims=True)
    share = jnp.concatenate([share, jnp.zeros((head - count - 1, head), jnp.float32)], axis=0).T
    merged = own[0, :rows, :].astype(jnp.float32) * share[:rows, count : count + 1]
    for part in range(count):
        merged += parts[part, :rows, :].astype(jnp.float32) * share[:rows, part : part + 1]
    merged = merged.astype(jnp.bfloat16)
    attention[...] = merged
    half = out.shape[1]
    other = pl.ds(pl.multiple_of((1 - place[2]) * half, half), half)
    out[...] = project(merged, hidden[:, other], weight[:, other], gain[:, other])


def merge(place, parts, own, hidden, weight, gain):
    rows, width = hidden.shape
    head = parts.shape[2]
    return pl.pallas_call(
        merge_kernel,
        out_shape=[
            jax.ShapeDtypeStruct((rows, head), jnp.bfloat16),
            jax.ShapeDtypeStruct((rows, width // 2), jnp.bfloat16),
        ],
        in_specs=[SMEM] + [VMEM] * 5,
        out_specs=[VMEM] * 2,
        compiler_params=pltpu.CompilerParams(vmem_limit_bytes=12 << 20),
        name="merge",
    )(place, parts, own, hidden, weight, gain)


def own_kernel(place, attention, hidden, weight, gain, out):
    half = out.shape[1]
    mine = pl.ds(pl.multiple_of(place[2] * half, half), half)
    out[...] = project(attention[...], hidden[:, mine], weight[:, mine], gain[:, mine])


def own_half(place, attention, hidden, weight, gain):
    rows, width = hidden.shape
    head = attention.shape[1]
    half = width // 2
    return pl.pallas_call(
        own_kernel,
        out_shape=jax.ShapeDtypeStruct((rows, half), jnp.bfloat16),
        in_specs=[SMEM] + [VMEM] * 4,
        out_specs=VMEM,
        cost_estimate=pl.CostEstimate(
            flops=2 * rows * head * half, bytes_accessed=4 * rows * half, transcendentals=0
        ),
        compiler_params=pltpu.CompilerParams(vmem_limit_bytes=12 << 20),
        name="own_half",
    )(place, attention, hidden, weight, gain)


def exchanged(blocks, axes):
    return lax.all_to_all(blocks, axes, 0, 0)


def spread(block, axes):
    return jnp.broadcast_to(block[None], (lax.axis_size(axes),) + block.shape)


def on_device(
    queries, fresh_keys, fresh_values, stale_keys, stale_values, hidden, out_weight, modulation
):
    side = lax.axis_index("guide")
    place = jnp.stack(
        [lax.axis_index(QUERY_AXES), lax.axis_index(KEY_AXES), side]
    ).astype(jnp.int32)
    query = queries[0]
    residual = hidden[0]
    gain = modulation[None, :]
    cached = jnp.concatenate([stale_keys[0], stale_values[0]], axis=1)
    fresh = jnp.concatenate([fresh_keys[0], fresh_values[0]], axis=1)
    query_blocks = spread(query, QUERY_AXES)
    group_queries = exchanged(query_blocks, QUERY_AXES)
    group_cached = lax.all_gather(cached, KEY_AXES, axis=0, tiled=True)
    keys, values = prepare(group_cached)
    partials = attend(group_queries, keys, values)
    parts = exchanged(partials, QUERY_AXES)
    own_part = attend_own(place, query, keys, values, fresh)
    attention, sent = merge(place, parts, own_part, residual, out_weight, gain)
    partner = lax.ppermute(sent, "guide", [(0, 1), (1, 0)])
    own = own_half(place, attention, residual, out_weight, gain)
    own_value = own.astype(jnp.float32)
    partner_value = partner.astype(jnp.float32)
    conditional = jnp.where(side == 0, own_value, partner_value)
    unconditional = jnp.where(side == 0, partner_value, own_value)
    guided = unconditional + GUIDANCE * (conditional - unconditional)
    return guided.astype(jnp.bfloat16)


def solution(mesh):
    split = Mesh(mesh.devices.reshape((mesh.shape["guide"],) + SIZES), ("guide",) + AXES)
    rows = P("guide", AXES, None)
    return jax.shard_map(
        on_device,
        mesh=split,
        in_specs=(rows,) * 6 + (P(), P()),
        out_specs=P(AXES, "guide"),
        check_vma=False,
    )
```

```python
import math

import jax
import jax.numpy as jnp
from jax import lax
from jax.experimental import pallas as pl
from jax.experimental.pallas import tpu as pltpu
from jax.sharding import Mesh
from jax.sharding import PartitionSpec as P

GUIDANCE = 5.0
AXES = ("x", "y", "z")
SIZES = (4, 4, 16)
QUERY_AXES = ("x", "y")
KEY_AXES = ("z",)
STATS = 8
TOGETHER = 4
VMEM = pl.BlockSpec(memory_space=pltpu.VMEM)


def position(axes):
    index = 0
    for axis in axes:
        index = index * lax.axis_size(axis) + lax.axis_index(axis)
    return index


def write_part(out, index, summed, total, peak, scale):
    rows, head = summed.shape
    out[index, :rows, :] = (summed / total).astype(out.dtype)
    level = peak * scale + jnp.log(total)
    level = jnp.concatenate([level, jnp.zeros((head - rows, head), jnp.float32)], axis=0)
    level = level.T[:STATS]
    high = level.astype(jnp.bfloat16).astype(jnp.float32)
    middle = (level - high).astype(jnp.bfloat16).astype(jnp.float32)
    low = level - high - middle
    row = lax.broadcasted_iota(jnp.int32, level.shape, 0)
    stats = jnp.where(row == 0, high, jnp.where(row == 1, middle, low))
    out[index, rows:, :] = stats.astype(out.dtype)


def prepare_kernel(cached, keys, values):
    head = keys.shape[0]
    keys[...] = cached[:, :head].T
    values[:, :head] = cached[:, head:]
    values[:, head:] = jnp.ones((values.shape[0], head), values.dtype)


def prepare(cached):
    rows, width = cached.shape
    return pl.pallas_call(
        prepare_kernel,
        out_shape=[
            jax.ShapeDtypeStruct((width // 2, rows), cached.dtype),
            jax.ShapeDtypeStruct((rows, width), cached.dtype),
        ],
        in_specs=[VMEM],
        out_specs=[VMEM] * 2,
        compiler_params=pltpu.CompilerParams(vmem_limit_bytes=12 << 20),
        name="prepare",
    )(cached)


def attend_own(query, keys, values, fresh, out):
    rows, head = query.shape
    scale = 1.0 / math.sqrt(head)
    contract = (((1,), (1,)), ((), ()))
    stale = jnp.dot(query[...], keys[...], preferred_element_type=jnp.float32)
    column = lax.broadcasted_iota(jnp.int32, stale.shape, 1) - position(KEY_AXES) * rows
    stale = jnp.where((column >= 0) & (column < rows), -jnp.inf, stale)
    new = lax.dot_general(
        query[...], fresh[:, :head], contract, preferred_element_type=jnp.float32
    )
    peak = jnp.maximum(
        jnp.max(stale, axis=1, keepdims=True), jnp.max(new, axis=1, keepdims=True)
    )
    factor = scale * math.log2(math.e)
    stale = jnp.exp2((stale - peak) * factor).astype(jnp.bfloat16)
    new = jnp.exp2((new - peak) * factor).astype(jnp.bfloat16)
    both = jnp.dot(stale, values[...], preferred_element_type=jnp.float32)
    total = both[:, head:] + jnp.sum(new.astype(jnp.float32), axis=1, keepdims=True)
    summed = both[:, :head] + jnp.dot(new, fresh[:, head:], preferred_element_type=jnp.float32)
    write_part(out, 0, summed, total, peak, scale)


def attend_kernel(query, keys, values, own_query, fresh, out, own):
    count, rows, head = query.shape
    scale = 1.0 / math.sqrt(head)
    for first in range(0, count, TOGETHER):
        block = query[first : first + TOGETHER].reshape(TOGETHER * rows, head)
        scores = jnp.dot(block, keys[...], preferred_element_type=jnp.float32)
        peak = jnp.max(scores, axis=1, keepdims=True)
        weights = jnp.exp2((scores - peak) * (scale * math.log2(math.e))).astype(jnp.bfloat16)
        summed = jnp.dot(weights, values[...], preferred_element_type=jnp.float32)
        for k in range(TOGETHER):
            part = slice(k * rows, (k + 1) * rows)
            write_part(out, first + k, summed[part, :head], summed[part, head:], peak[part], scale)
    attend_own(own_query, keys, values, fresh, own)


def attend(queries, keys, values, own_query, fresh):
    count, rows, head = queries.shape
    size = count * rows * keys.shape[1]
    return pl.pallas_call(
        attend_kernel,
        out_shape=[
            jax.ShapeDtypeStruct((count, rows + STATS, head), jnp.bfloat16),
            jax.ShapeDtypeStruct((1, rows + STATS, head), jnp.bfloat16),
        ],
        in_specs=[VMEM] * 5,
        out_specs=[VMEM] * 2,
        cost_estimate=pl.CostEstimate(
            flops=6 * size * head, bytes_accessed=8 * keys.size, transcendentals=size
        ),
        compiler_params=pltpu.CompilerParams(vmem_limit_bytes=24 << 20),
        name="attend",
    )(queries, keys, values, own_query, fresh)


def project(attention, hidden, weight, gain):
    projected = jnp.dot(attention, weight, preferred_element_type=jnp.float32)
    return (hidden.astype(jnp.float32) + gain * projected).astype(jnp.bfloat16)


def level_of(part, rows):
    pieces = part[rows:, :].astype(jnp.float32)
    return pieces[0:1] + pieces[1:2] + pieces[2:3]


def merge_kernel(parts, own, hidden, weight, gain, attention, out):
    count = parts.shape[0]
    rows, head = attention.shape
    mine = position(QUERY_AXES)
    levels = []
    for part in range(count):
        level = level_of(parts[part], rows)
        levels.append(jnp.where(mine == part, -jnp.inf, level))
    levels.append(level_of(own[0], rows))
    level = jnp.concatenate(levels, axis=0)
    share = jnp.exp(level - jnp.max(level, axis=0, keepdims=True))
    share = share / jnp.sum(share, axis=0, keepdims=True)
    share = jnp.concatenate([share, jnp.zeros((head - count - 1, head), jnp.float32)], axis=0).T
    merged = own[0, :rows, :].astype(jnp.float32) * share[:rows, count : count + 1]
    for part in range(count):
        merged += parts[part, :rows, :].astype(jnp.float32) * share[:rows, part : part + 1]
    merged = merged.astype(jnp.bfloat16)
    attention[...] = merged
    half = out.shape[1]
    other = pl.ds(pl.multiple_of((1 - lax.axis_index("guide")) * half, half), half)
    out[...] = project(merged, hidden[:, other], weight[:, other], gain[:, other])


def merge(parts, own, hidden, weight, gain):
    rows, width = hidden.shape
    return pl.pallas_call(
        merge_kernel,
        out_shape=[
            jax.ShapeDtypeStruct((rows, own.shape[2]), jnp.bfloat16),
            jax.ShapeDtypeStruct((rows, width // 2), jnp.bfloat16),
        ],
        in_specs=[VMEM] * 5,
        out_specs=[VMEM] * 2,
        compiler_params=pltpu.CompilerParams(vmem_limit_bytes=8 << 20),
        name="merge",
    )(parts, own, hidden, weight, gain)


def own_kernel(attention, hidden, weight, gain, out):
    half = out.shape[1]
    mine = pl.ds(pl.multiple_of(lax.axis_index("guide") * half, half), half)
    out[...] = project(attention[...], hidden[:, mine], weight[:, mine], gain[:, mine])


def own_half(attention, hidden, weight, gain):
    rows, width = hidden.shape
    head = attention.shape[1]
    half = width // 2
    return pl.pallas_call(
        own_kernel,
        out_shape=jax.ShapeDtypeStruct((rows, half), jnp.bfloat16),
        in_specs=[VMEM] * 4,
        out_specs=VMEM,
        cost_estimate=pl.CostEstimate(
            flops=2 * rows * head * half, bytes_accessed=4 * rows * half, transcendentals=0
        ),
        compiler_params=pltpu.CompilerParams(vmem_limit_bytes=8 << 20),
        name="own_half",
    )(attention, hidden, weight, gain)


def guide_kernel(own, partner, out):
    first = lax.axis_index("guide") == 0
    own_value = own[...].astype(jnp.float32)
    partner_value = partner[...].astype(jnp.float32)
    conditional = jnp.where(first, own_value, partner_value)
    unconditional = jnp.where(first, partner_value, own_value)
    guided = unconditional + GUIDANCE * (conditional - unconditional)
    out[...] = guided.astype(out.dtype)


def guide(own, partner):
    return pl.pallas_call(
        guide_kernel,
        out_shape=jax.ShapeDtypeStruct(own.shape, own.dtype),
        in_specs=[VMEM] * 2,
        out_specs=VMEM,
        compiler_params=pltpu.CompilerParams(vmem_limit_bytes=8 << 20),
        name="guide",
    )(own, partner)


def start_kernel(query, keys, values, new_keys, new_values, blocks, cached, fresh, held, done):
    head = query.shape[1]
    copies = [
        pltpu.make_async_copy(query, held, done.at[0]),
        pltpu.make_async_copy(keys, cached.at[:, :head], done.at[1]),
        pltpu.make_async_copy(values, cached.at[:, head:], done.at[2]),
        pltpu.make_async_copy(new_keys, fresh.at[:, :head], done.at[3]),
        pltpu.make_async_copy(new_values, fresh.at[:, head:], done.at[4]),
    ]
    for copy in copies:
        copy.start()
    copies[0].wait()
    for block in range(blocks.shape[0]):
        blocks[block] = held[...]
    for copy in copies[1:]:
        copy.wait()


def start(query, keys, values, new_keys, new_values):
    rows, head = query.shape
    count = lax.axis_size(QUERY_AXES)
    wide = jax.ShapeDtypeStruct((rows, 2 * head), query.dtype)
    return pl.pallas_call(
        start_kernel,
        out_shape=[jax.ShapeDtypeStruct((count, rows, head), query.dtype), wide, wide],
        in_specs=[pl.BlockSpec(memory_space=pltpu.HBM)] * 5,
        out_specs=[VMEM] * 3,
        scratch_shapes=[pltpu.VMEM((rows, head), query.dtype), pltpu.SemaphoreType.DMA((5,))],
        compiler_params=pltpu.CompilerParams(vmem_limit_bytes=60 << 20),
        name="start",
    )(query, keys, values, new_keys, new_values)


def exchanged(blocks, axes):
    return lax.all_to_all(blocks, axes, 0, 0)


def on_device(
    queries, fresh_keys, fresh_values, stale_keys, stale_values, hidden, out_weight, modulation
):
    query = queries[0]
    residual = hidden[0]
    gain = modulation[None, :]
    query_blocks, cached, fresh = start(
        query, stale_keys[0], stale_values[0], fresh_keys[0], fresh_values[0]
    )
    group_queries = exchanged(query_blocks, QUERY_AXES)
    group_cached = lax.all_gather(cached, KEY_AXES, axis=0, tiled=True)
    keys, values = prepare(group_cached)
    partials, own_part = attend(group_queries, keys, values, query, fresh)
    parts = exchanged(partials, QUERY_AXES)
    attention, sent = merge(parts, own_part, residual, out_weight, gain)
    partner = lax.ppermute(sent, "guide", [(0, 1), (1, 0)])
    own = own_half(attention, residual, out_weight, gain)
    return guide(own, partner)


def solution(mesh):
    split = Mesh(mesh.devices.reshape((mesh.shape["guide"],) + SIZES), ("guide",) + AXES)
    rows = P("guide", AXES, None)
    return jax.shard_map(
        on_device,
        mesh=split,
        in_specs=(rows,) * 6 + (P(), P()),
        out_specs=P(AXES, "guide"),
        check_vma=False,
    )
```

```python
import math

import jax
import jax.numpy as jnp
from jax import lax
from jax.experimental import pallas as pl
from jax.experimental.pallas import tpu as pltpu
from jax.sharding import Mesh
from jax.sharding import PartitionSpec as P

GUIDANCE = 5.0
AXES = ("x", "y", "z")
SIZES = (4, 4, 16)
QUERY_AXES = ("x", "y")
KEY_AXES = ("z",)
STATS = 8
TOGETHER = 2
VMEM = pl.BlockSpec(memory_space=pltpu.VMEM)


def position(axes):
    index = 0
    for axis in axes:
        index = index * lax.axis_size(axis) + lax.axis_index(axis)
    return index


def write_part(out, index, summed, total, peak, scale):
    rows, head = summed.shape
    out[index, :rows, :] = (summed / total).astype(out.dtype)
    level = peak * scale + jnp.log(total)
    level = jnp.concatenate([level, jnp.zeros((head - rows, head), jnp.float32)], axis=0)
    level = level.T[:STATS]
    high = level.astype(jnp.bfloat16).astype(jnp.float32)
    middle = (level - high).astype(jnp.bfloat16).astype(jnp.float32)
    low = level - high - middle
    row = lax.broadcasted_iota(jnp.int32, level.shape, 0)
    stats = jnp.where(row == 0, high, jnp.where(row == 1, middle, low))
    out[index, rows:, :] = stats.astype(out.dtype)


def attend_own(query, keys, values, new_keys, new_values, out):
    rows, head = query.shape
    scale = 1.0 / math.sqrt(head)
    contract = (((1,), (1,)), ((), ()))
    stale = jnp.dot(query[...], keys[...], preferred_element_type=jnp.float32)
    column = lax.broadcasted_iota(jnp.int32, stale.shape, 1) - position(KEY_AXES) * rows
    stale = jnp.where((column >= 0) & (column < rows), -jnp.inf, stale)
    new = lax.dot_general(
        query[...], new_keys[...], contract, preferred_element_type=jnp.float32
    )
    peak = jnp.maximum(
        jnp.max(stale, axis=1, keepdims=True), jnp.max(new, axis=1, keepdims=True)
    )
    factor = scale * math.log2(math.e)
    stale = jnp.exp2((stale - peak) * factor).astype(jnp.bfloat16)
    new = jnp.exp2((new - peak) * factor).astype(jnp.bfloat16)
    both = jnp.dot(stale, values[...], preferred_element_type=jnp.float32)
    total = both[:, head:] + jnp.sum(new.astype(jnp.float32), axis=1, keepdims=True)
    summed = both[:, :head] + jnp.dot(new, new_values[...], preferred_element_type=jnp.float32)
    write_part(out, 0, summed, total, peak, scale)


def attend_kernel(query, cached, own_query, new_keys, new_values, out, own, keys, values):
    count, rows, head = query.shape
    keys[...] = cached[:, :head].T
    values[:, :head] = cached[:, head:]
    values[:, head:] = jnp.ones((values.shape[0], head), values.dtype)
    scale = 1.0 / math.sqrt(head)
    for first in range(0, count, TOGETHER):
        block = query[first : first + TOGETHER].reshape(TOGETHER * rows, head)
        scores = jnp.dot(block, keys[...], preferred_element_type=jnp.float32)
        peak = jnp.max(scores, axis=1, keepdims=True)
        weights = jnp.exp2((scores - peak) * (scale * math.log2(math.e))).astype(jnp.bfloat16)
        summed = jnp.dot(weights, values[...], preferred_element_type=jnp.float32)
        for k in range(TOGETHER):
            part = slice(k * rows, (k + 1) * rows)
            write_part(out, first + k, summed[part, :head], summed[part, head:], peak[part], scale)
    attend_own(own_query, keys, values, new_keys, new_values, own)


def attend(queries, cached, own_query, new_keys, new_values):
    count, rows, head = queries.shape
    keys = cached.shape[0]
    size = count * rows * keys
    return pl.pallas_call(
        attend_kernel,
        out_shape=[
            jax.ShapeDtypeStruct((count, rows + STATS, head), jnp.bfloat16),
            jax.ShapeDtypeStruct((1, rows + STATS, head), jnp.bfloat16),
        ],
        in_specs=[VMEM] * 5,
        out_specs=[VMEM] * 2,
        scratch_shapes=[
            pltpu.VMEM((head, keys), cached.dtype),
            pltpu.VMEM((keys, 2 * head), cached.dtype),
        ],
        cost_estimate=pl.CostEstimate(
            flops=6 * size * head, bytes_accessed=4 * cached.size, transcendentals=size
        ),
        compiler_params=pltpu.CompilerParams(vmem_limit_bytes=24 << 20),
        name="attend",
    )(queries, cached, own_query, new_keys, new_values)


def project(attention, hidden, weight, gain):
    projected = jnp.dot(attention, weight, preferred_element_type=jnp.float32)
    return (hidden.astype(jnp.float32) + gain * projected).astype(jnp.bfloat16)


def level_of(part, rows):
    pieces = part[rows:, :].astype(jnp.float32)
    return pieces[0:1] + pieces[1:2] + pieces[2:3]


def merge_kernel(parts, own, hidden, weight, gain, attention, out):
    count = parts.shape[0]
    rows, head = attention.shape
    mine = position(QUERY_AXES)
    levels = []
    for part in range(count):
        level = level_of(parts[part], rows)
        levels.append(jnp.where(mine == part, -jnp.inf, level))
    levels.append(level_of(own[0], rows))
    level = jnp.concatenate(levels, axis=0)
    share = jnp.exp(level - jnp.max(level, axis=0, keepdims=True))
    share = share / jnp.sum(share, axis=0, keepdims=True)
    share = jnp.concatenate([share, jnp.zeros((head - count - 1, head), jnp.float32)], axis=0).T
    merged = own[0, :rows, :].astype(jnp.float32) * share[:rows, count : count + 1]
    for part in range(count):
        merged += parts[part, :rows, :].astype(jnp.float32) * share[:rows, part : part + 1]
    merged = merged.astype(jnp.bfloat16)
    attention[...] = merged
    half = out.shape[1]
    other = pl.ds(pl.multiple_of((1 - lax.axis_index("guide")) * half, half), half)
    out[...] = project(merged, hidden[:, other], weight[:, other], gain[:, other])


def merge(parts, own, hidden, weight, gain):
    rows, width = hidden.shape
    return pl.pallas_call(
        merge_kernel,
        out_shape=[
            jax.ShapeDtypeStruct((rows, own.shape[2]), jnp.bfloat16),
            jax.ShapeDtypeStruct((rows, width // 2), jnp.bfloat16),
        ],
        in_specs=[VMEM] * 5,
        out_specs=[VMEM] * 2,
        compiler_params=pltpu.CompilerParams(vmem_limit_bytes=8 << 20),
        name="merge",
    )(parts, own, hidden, weight, gain)


def own_kernel(attention, hidden, weight, gain, out):
    half = out.shape[1]
    mine = pl.ds(pl.multiple_of(lax.axis_index("guide") * half, half), half)
    out[...] = project(attention[...], hidden[:, mine], weight[:, mine], gain[:, mine])


def own_half(attention, hidden, weight, gain):
    rows, width = hidden.shape
    head = attention.shape[1]
    half = width // 2
    return pl.pallas_call(
        own_kernel,
        out_shape=jax.ShapeDtypeStruct((rows, half), jnp.bfloat16),
        in_specs=[VMEM] * 4,
        out_specs=VMEM,
        cost_estimate=pl.CostEstimate(
            flops=2 * rows * head * half, bytes_accessed=4 * rows * half, transcendentals=0
        ),
        compiler_params=pltpu.CompilerParams(vmem_limit_bytes=8 << 20),
        name="own_half",
    )(attention, hidden, weight, gain)


def guide_kernel(own, partner, out):
    first = lax.axis_index("guide") == 0
    own_value = own[...].astype(jnp.float32)
    partner_value = partner[...].astype(jnp.float32)
    conditional = jnp.where(first, own_value, partner_value)
    unconditional = jnp.where(first, partner_value, own_value)
    guided = unconditional + GUIDANCE * (conditional - unconditional)
    out[...] = guided.astype(out.dtype)


def guide(own, partner):
    return pl.pallas_call(
        guide_kernel,
        out_shape=jax.ShapeDtypeStruct(own.shape, own.dtype),
        in_specs=[VMEM] * 2,
        out_specs=VMEM,
        compiler_params=pltpu.CompilerParams(vmem_limit_bytes=8 << 20),
        name="guide",
    )(own, partner)


def start_kernel(query, keys, values, blocks, cached, held, done):
    head = query.shape[1]
    copies = [
        pltpu.make_async_copy(query, held, done.at[0]),
        pltpu.make_async_copy(keys, cached.at[:, :head], done.at[1]),
        pltpu.make_async_copy(values, cached.at[:, head:], done.at[2]),
    ]
    for copy in copies:
        copy.start()
    copies[0].wait()
    for block in range(blocks.shape[0]):
        blocks[block] = held[...]
    for copy in copies[1:]:
        copy.wait()


def start(query, keys, values):
    rows, head = query.shape
    count = lax.axis_size(QUERY_AXES)
    wide = jax.ShapeDtypeStruct((rows, 2 * head), query.dtype)
    return pl.pallas_call(
        start_kernel,
        out_shape=[jax.ShapeDtypeStruct((count, rows, head), query.dtype), wide],
        in_specs=[pl.BlockSpec(memory_space=pltpu.HBM)] * 3,
        out_specs=[VMEM] * 2,
        scratch_shapes=[pltpu.VMEM((rows, head), query.dtype), pltpu.SemaphoreType.DMA((3,))],
        compiler_params=pltpu.CompilerParams(vmem_limit_bytes=60 << 20),
        name="start",
    )(query, keys, values)


def exchanged(blocks, axes):
    return lax.all_to_all(blocks, axes, 0, 0)


def on_device(
    queries, fresh_keys, fresh_values, stale_keys, stale_values, hidden, out_weight, modulation
):
    query = queries[0]
    residual = hidden[0]
    gain = modulation[None, :]
    query_blocks, cached = start(query, stale_keys[0], stale_values[0])
    group_queries = exchanged(query_blocks, QUERY_AXES)
    group_cached = lax.all_gather(cached, KEY_AXES, axis=0, tiled=True)
    partials, own_part = attend(group_queries, group_cached, query, fresh_keys[0], fresh_values[0])
    parts = exchanged(partials, QUERY_AXES)
    attention, sent = merge(parts, own_part, residual, out_weight, gain)
    partner = lax.ppermute(sent, "guide", [(0, 1), (1, 0)])
    own = own_half(attention, residual, out_weight, gain)
    return guide(own, partner)


def solution(mesh):
    split = Mesh(mesh.devices.reshape((mesh.shape["guide"],) + SIZES), ("guide",) + AXES)
    rows = P("guide", AXES, None)
    return jax.shard_map(
        on_device,
        mesh=split,
        in_specs=(rows,) * 6 + (P(), P()),
        out_specs=P(AXES, "guide"),
        check_vma=False,
    )
```
